32 devices in a mesh: groups: 2 (over y), tensor: 4 (over z), section: 4 (over x, core).
Axes of the slice: x: 2, y: 2, z: 4, core: 2. Of those that a mesh axis runs over, the one named last changes fastest.
Arguments:
- inputs: bfloat16 [4, 64, 8192], P('groups', None, 'tensor'), parts along dimension 0, may hold values from -6 to 6
- gains: bfloat16 [4, 8192], P('section'), may hold values from 0.099609375 to 1.8984375
- keep_mask: int32 [4, 128, 128], P('section', 'tensor'), may hold values from 0 to 1, as said below
- block_values: bfloat16 [4, 12288, 4096], P('section', 'tensor'), may hold values from -0.09375 to 0.09375
- head: bfloat16 [32000, 8192], P(('tensor', 'section')), may hold values from -30 to 30
- targets: int32 [4, 64], P('groups'), parts along dimension 0, may hold values from 0 to 31999
Outputs:
- token_loss: float32 [4, 64], P('groups'), parts along dimension 0
- mean_loss: float32 [2], P('groups'), parts along dimension 0
The draws below stay inside these ranges and needn't reach their ends.
There are 2 independent parts, one for each index of `groups`. The reference program is written for one: setup_inputs(seed, part) draws one part's arguments, and reference() takes and returns one part's arrays. A program takes and returns all parts, laid end to end along the dimension named above; an argument that names none is the same for every part. Nothing has to cross between parts.
Inputs may be any that keep to these rules, and one draw needn't show every extreme that they name: `keep_mask`: in each section, band t (block rows t * 32 to (t + 1) * 32 - 1) keeps between 1024 and 3072 blocks, and some band of each section keeps exactly 3072. List slots past a band's count of kept blocks are not read.
All inputs are finite; a program needn't handle non-finite values.
Results may differ from the reference program's by a relative error of at most 0.0044.
The reference program's roundings to bfloat16 on the way count: a program that leaves them out, or rounds other values in their place, can miss the bound.
Values may be sent and summed in bfloat16 or wider, within the bound.
A program may use at most 320 MiB of HBM per device.

```python
import math
import jax
import jax.numpy as jnp
import numpy as np
from jax import lax

D = 8192
VOCAB = 32000
BLK = 64
MICRO = 2
MB = 64
SECTIONS = 4
NB = 128
RB = 32
BAND = 4096
NBMAX = 3072
N_TENSOR = 4


def draw_keep_mask(key, part):
    key_count, key_extra, key_most, key_order = jax.random.split(key, 4)
    quarter = BAND // 4
    counts = quarter + jax.random.randint(key_count, (SECTIONS, N_TENSOR), 0, quarter + 1) + jax.random.randint(key_extra, (SECTIONS, N_TENSOR), 0, quarter + 1)
    fullest = jax.random.randint(key_most, (SECTIONS, 1), 0, N_TENSOR)
    counts = jnp.where(jnp.arange(N_TENSOR)[None, :] == fullest, NBMAX, counts)
    order_keys = jax.random.split(key_order, SECTIONS * N_TENSOR)
    orders = jax.vmap(lambda subkey: jax.random.permutation(subkey, BAND))(order_keys)
    ranks = jnp.argsort(orders, axis=1)
    kept = (ranks < counts.reshape(-1, 1)).astype(jnp.int32)
    return kept.reshape(SECTIONS, NB, NB)


def draw_head(key, part):
    key_base = jax.random.fold_in(key, 0)
    key_jitter = jax.random.fold_in(key, 5)
    spread = 1.0 / math.sqrt(D)
    position = jnp.arange(VOCAB, dtype=jnp.float32)[:, None] / VOCAB
    jitter = jnp.exp(jax.random.uniform(key_jitter, (VOCAB, 1), jnp.float32, 0.0, math.log(1.5)))
    row_scale = 0.8 * jnp.exp(position * math.log(10.0)) * jitter
    base = jnp.clip(jax.random.normal(key_base, (VOCAB, D), jnp.float32), -6.0, 6.0) * spread * row_scale
    return base.astype(jnp.bfloat16)


def plant(result, key, smallest, largest):
    longest = result.shape.index(max(result.shape))
    spots = []
    for shift in (0, 1):
        where = [jax.random.randint(jax.random.fold_in(key, axis), (), 0, length) for axis, length in enumerate(result.shape)]
        where[longest] = (where[longest] + shift) % result.shape[longest]
        spots.append(tuple(where))
    return result.at[spots[0]].set(smallest).at[spots[1]].set(largest)


def block_levels(key, extent, pieces, least, top_value):
    level = 1.0
    for axis_at, blocks in pieces:
        steps = jax.random.uniform(jax.random.fold_in(jax.random.fold_in(key, 6), axis_at), (blocks,), jnp.float32, least / len(pieces), top_value / len(pieces))
        level = level * jnp.repeat(jnp.exp(steps), extent[axis_at] // blocks).reshape((-1,) + (1,) * (len(extent) - 1 - axis_at))
    return level


def cumulative_ranks(count, lean):
    loads = [(1 << 20) // math.isqrt(rank ** lean) + 1 for rank in range(1, count + 1)]
    scale = 1 + sum(loads) // (1 << 30)
    return np.cumsum(np.array([max(1, weight // scale) for weight in loads]))


def ranked_ids(stream_key, shape, count, lean):
    table = cumulative_ranks(count, lean)
    ticket = jax.random.randint(jax.random.fold_in(stream_key, 1), shape, 0, int(table[count - 1]))
    rank = jnp.searchsorted(jnp.asarray(table, jnp.int32), ticket, side="right")
    return jax.random.permutation(jax.random.fold_in(stream_key, 2), count)[rank].astype(jnp.int32)


def centred(own_key, extent, width, most, cuts=(), held_as=jnp.bfloat16):
    array = width * jax.random.normal(own_key, extent, jnp.float32)
    if cuts:
        array = array * block_levels(own_key, extent, cuts, -0.22, 0.18)
    return jnp.clip(array, -most, most).astype(held_as)


def setup_inputs(seed: int = 0, part: int = 0) -> dict:
    streams_of = jax.random.split(jax.random.key(seed), 7)
    own_keys = jax.random.split(jax.random.fold_in(streams_of[6], part), 7)
    return {
        "inputs": centred(own_keys[0], (MICRO, MB, D), 1.0, 6.0, ((2, 4),)),
        "gains": jnp.clip(1.0 + 0.18 * jax.random.normal(streams_of[1], (SECTIONS, D), jnp.float32), 0.099609375, 1.8984375).astype(jnp.bfloat16),
        "keep_mask": draw_keep_mask(jax.random.fold_in(streams_of[6], 71), part),
        "block_values": centred(streams_of[3], (SECTIONS, N_TENSOR * NBMAX, BLK * BLK), (D // 2) ** -0.5, 0.09375, ((0, 4), (1, 4))),
        "head": draw_head(jax.random.fold_in(streams_of[6], 71), part),
        "targets": plant(ranked_ids(own_keys[5], (MICRO, MB), VOCAB, 2), jax.random.fold_in(own_keys[5], 3), 0, VOCAB - 1).astype(jnp.int32),
    }


epsilon = 1e-05

def section_weight(mask_section, values_section):
    flat_mask = mask_section.reshape(N_TENSOR, BAND)
    slots = jnp.cumsum(flat_mask, axis=1, dtype=jnp.int32) - 1
    slots = jnp.clip(slots, 0, NBMAX - 1).astype(jnp.int32)
    lists = values_section.reshape(N_TENSOR, NBMAX, BLK * BLK)
    picked = jax.vmap(lambda table, where: table[where])(lists, slots)
    picked = picked * flat_mask[:, :, None].astype(jnp.bfloat16)
    blocks = picked.reshape(N_TENSOR, RB, NB, BLK, BLK)
    return blocks.transpose(0, 1, 3, 2, 4).reshape(D, D)

def reference(inputs, gains, keep_mask, block_values, head, targets):
    hidden = inputs.reshape(MICRO * MB, D)
    for section_number in range(SECTIONS):
        weight_matrix = section_weight(keep_mask[section_number], block_values[section_number])
        wide = hidden.astype(jnp.float32)
        sumsq = lax.optimization_barrier(jnp.sum(wide * wide, axis=1, keepdims=True))
        scaled = (wide * gains[section_number].astype(jnp.float32)).astype(jnp.bfloat16)
        product = jnp.dot(scaled, weight_matrix, preferred_element_type=jnp.float32)
        hidden = (wide + product * lax.rsqrt(sumsq / D + epsilon)).astype(jnp.bfloat16)
    wide = hidden.astype(jnp.float32)
    final_sumsq = lax.optimization_barrier(jnp.sum(wide * wide, axis=1, keepdims=True))
    logits = jnp.dot(hidden, head.T, preferred_element_type=jnp.float32) * lax.rsqrt(final_sumsq / D + epsilon)
    top = lax.optimization_barrier(jnp.max(logits, axis=1))
    total = lax.optimization_barrier(jnp.sum(jnp.exp(logits - top[:, None]), axis=1))
    flat_targets = targets.reshape(-1).astype(jnp.int32)
    chosen = jnp.take_along_axis(logits, flat_targets[:, None], axis=1)[:, 0]
    token_loss = (top + jnp.log(total) - chosen).reshape(MICRO, MB)
    mean_loss = jnp.mean(token_loss).reshape(1)
    return (token_loss, mean_loss)
```

```python
import jax
import jax.numpy as jnp
from jax import lax
from jax.experimental import pallas as pl
from jax.experimental.pallas import tpu as pltpu
from jax.sharding import PartitionSpec as P

D = 8192
BLK = 64
PAIR = 2 * BLK
HALF = BLK // 2

epsilon = 1e-05


def shifted(block, axis, distance):
    devices = range(lax.axis_size(axis))
    route = [(i - distance, i) for i in devices if i - distance in devices]
    return lax.ppermute(block, axis, route)


def build_body(block_count, index_ref, start_ref, window_ref, panel_ref):
    row = pl.program_id(0)
    start = start_ref[row]
    for column in range(block_count):
        slot = index_ref[row * block_count + column]
        near = jnp.clip(slot - start, 0, window_ref.shape[0] - 1)
        keep = jnp.where(slot >= 0, 1.0, 0.0).astype(jnp.float32)
        factor = jnp.full((HALF, PAIR), keep, jnp.float32).astype(jnp.bfloat16)
        panel_ref[:, column * PAIR : (column + 1) * PAIR] = window_ref[near] * factor


def build_panel(mask, values):
    band_rows, block_count = mask.shape
    slot_count = values.shape[0]
    running = jnp.cumsum(mask.reshape(-1), dtype=jnp.int32)
    slots = jnp.clip(running - 1, 0, slot_count - 1)
    index = jnp.where(mask.reshape(-1) > 0, slots, -1)
    before = running.reshape(band_rows, block_count)[:, 0] - mask[:, 0]
    window = min(block_count, slot_count)
    starts = jnp.clip(before, 0, slot_count - window).astype(jnp.int32)
    lists = values.reshape(slot_count, HALF, PAIR)
    spec = pltpu.PrefetchScalarGridSpec(
        num_scalar_prefetch=2,
        grid=(band_rows,),
        in_specs=[
            pl.BlockSpec(
                (pl.Element(window), pl.Element(HALF), pl.Element(PAIR)),
                lambda r, index_ref, start_ref: (start_ref[r], 0, 0),
            )
        ],
        out_specs=pl.BlockSpec((HALF, block_count * PAIR), lambda r, *_: (r, 0)),
    )

    def body(*refs):
        build_body(block_count, *refs)

    return pl.pallas_call(
        body,
        grid_spec=spec,
        out_shape=jax.ShapeDtypeStruct((band_rows * HALF, block_count * PAIR), jnp.bfloat16),
        compiler_params=pltpu.CompilerParams(
            dimension_semantics=("arbitrary",), vmem_limit_bytes=40 << 20
        ),
    )(index, starts, lists)


def joined_loss(logits_top, total, chosen):
    stacked = jnp.stack([logits_top, total, chosen])
    everything = lax.all_gather(stacked, ("tensor", "section"))
    tops = everything[:, 0]
    top = jnp.max(tops, axis=0)
    total = jnp.sum(everything[:, 1] * jnp.exp(tops - top[None, :]), axis=0)
    return top + jnp.log(total) - jnp.sum(everything[:, 2], axis=0)


def on_device(inputs, gains, keep_mask, block_values, head, targets):
    section_count = lax.axis_size("section")
    tensor_index = lax.axis_index("tensor")
    section_index = lax.axis_index("section")
    micro_count, row_count, local_width = inputs.shape
    rows = micro_count * row_count
    panel = build_panel(keep_mask[0], block_values[0])
    gain = lax.dynamic_slice(gains[0], (tensor_index * local_width,), (local_width,))
    gain = gain.astype(jnp.float32)
    own = inputs.reshape(rows, local_width)
    incoming = own
    low = (jnp.arange(PAIR) < BLK)[None, None, :]
    for moment in range(section_count):
        current = jnp.where(section_index == 0, own, incoming) if moment else own
        wide = current.astype(jnp.float32)
        sumsq = lax.psum(jnp.sum(wide * wide, axis=1), "tensor")
        scaled = (wide * gain).astype(jnp.bfloat16)
        split = scaled.reshape(rows, local_width // 2, 2).transpose(2, 0, 1)
        both = jnp.dot(
            split.reshape(2 * rows, local_width // 2), panel, preferred_element_type=jnp.float32
        ).reshape(2, rows, D // BLK, PAIR)
        partial = (both[0, :, :, :BLK] + both[1, :, :, BLK:]).reshape(rows, D)
        product = lax.psum_scatter(partial, "tensor", scatter_dimension=1, tiled=True)
        update = product * lax.rsqrt(sumsq[:, None] / D + epsilon)
        outgoing = (wide + update).astype(jnp.bfloat16)
        if moment < section_count - 1:
            incoming = shifted(outgoing, "section", 1)
    vocab_rows = head.shape[0]
    final = jnp.where(section_index == section_count - 1, outgoing, jnp.zeros_like(outgoing))
    relayed = lax.psum(final, "section")
    portion = lax.all_gather(relayed, "tensor", axis=1, tiled=True)
    raw_logits = lax.dot_general(
        portion, head, (((1,), (1,)), ((), ())), preferred_element_type=jnp.float32
    )
    widened = portion.astype(jnp.float32)
    final_sumsq = jnp.sum(widened * widened, axis=1)
    logits = raw_logits * lax.rsqrt(final_sumsq[:, None] / D + epsilon)
    vocab_start = (tensor_index * section_count + section_index) * vocab_rows
    local_ids = targets.reshape(-1) - vocab_start
    matches = jnp.arange(vocab_rows, dtype=jnp.int32)[None, :] == local_ids[:, None]
    target_logit = jnp.sum(jnp.where(matches, logits, 0.0), axis=1)
    local_top = jnp.max(logits, axis=1)
    local_total = jnp.sum(jnp.exp(logits - local_top[:, None]), axis=1)
    losses = joined_loss(local_top, local_total, target_logit)
    token_loss = losses.reshape(micro_count, row_count)
    mean_loss = jnp.mean(token_loss).reshape(1)
    return (token_loss, mean_loss)


def solution(mesh):
    placed = (
        P("groups", None, "tensor"),
        P("section", None),
        P("section", "tensor", None),
        P("section", "tensor", None),
        P(("tensor", "section"), None),
        P("groups", None),
    )
    return jax.shard_map(
        on_device,
        mesh=mesh,
        in_specs=placed,
        out_specs=(P("groups", None), P("groups")),
        check_vma=False,
    )
```
